32 devices in a mesh: fsdp: 32 (over z, y, x, core).
Axes of the slice: x: 2, y: 2, z: 4, core: 2. Of those that a mesh axis runs over, the one named last changes fastest.
Arguments:
- inputs: bfloat16 [4096, 1024], P('fsdp'), may hold values from -9 to 9
- live_keys: int32 [4096], P('fsdp'), may hold values from 0 to 1, as said below
- triple_weight: bfloat16 [1024, 3072], P('fsdp'), may hold values from -1 to 1
- query_bias: bfloat16 [1024], P('fsdp'), may hold values from -3 to 3
- value_bias: bfloat16 [1024], P('fsdp'), may hold values from -3 to 3
- output_weight: bfloat16 [1024, 1024], P('fsdp'), may hold values from -1.5 to 1.5
- output_bias: bfloat16 [1024], P('fsdp'), may hold values from -3 to 3
- first_gain: bfloat16 [1024], P('fsdp'), may hold values from 0.5 to 1.5
- first_shift: bfloat16 [1024], P('fsdp'), may hold values from -3 to 3
- expand_weight: bfloat16 [1024, 4096], P('fsdp'), may hold values from -0.1875 to 0.1875
- expand_bias: bfloat16 [4096], P('fsdp'), may hold values from -3 to 3
- shrink_weight: bfloat16 [4096, 1024], P('fsdp'), may hold values from -0.09375 to 0.09375
- shrink_bias: bfloat16 [1024], P('fsdp'), may hold values from -3 to 3
- second_gain: bfloat16 [1024], P('fsdp'), may hold values from 0.5 to 1.5
- second_shift: bfloat16 [1024], P('fsdp'), may hold values from -3 to 3
- cotangent: bfloat16 [4096, 1024], P('fsdp'), may hold values from -6 to 6
Outputs:
- layer_out: bfloat16 [4096, 1024], P('fsdp')
- input_grad: bfloat16 [4096, 1024], P('fsdp')
- triple_grad: float32 [1024, 3072], P('fsdp')
- query_bias_grad: float32 [1024], P('fsdp')
- value_bias_grad: float32 [1024], P('fsdp')
- output_grad: float32 [1024, 1024], P('fsdp')
- output_bias_grad: float32 [1024], P('fsdp')
- first_gain_grad: float32 [1024], P('fsdp')
- first_shift_grad: float32 [1024], P('fsdp')
- expand_grad: float32 [1024, 4096], P('fsdp')
- expand_bias_grad: float32 [4096], P('fsdp')
- shrink_grad: float32 [4096, 1024], P('fsdp')
- shrink_bias_grad: float32 [1024], P('fsdp')
- second_gain_grad: float32 [1024], P('fsdp')
- second_shift_grad: float32 [1024], P('fsdp')
The draws below stay inside these ranges and needn't reach their ends.
Inputs may be any that keep to these rules, and one draw needn't show every extreme that they name: `live_keys`: on each device the live rows come first: 2 to 128 of its 128 rows are live, and some device has all 128 live.
All inputs are finite; a program needn't handle non-finite values.
Results may differ from the reference program's by a relative error of at most 0.013.
The reference program's roundings to bfloat16 on the way count: a program that leaves them out, or rounds other values in their place, can miss the bound.
Values may be sent and summed in bfloat16 or wider, within the bound.
A program may use at most 256 MiB of HBM per device.

```python
import jax
import jax.numpy as jnp
from jax import lax

D = 1024
FF = 4096
HEADS = 16
TOK_DEV = 128
TOKENS = 4096


def draw_live_keys(key, part):
    groups = TOKENS // TOK_DEV
    base = jax.random.fold_in(key, 11)
    length_key, chosen_key = jax.random.split(base)
    lengths = jax.random.randint(length_key, (groups,), 2, TOK_DEV + 1).astype(jnp.int32)
    chosen = jax.random.randint(chosen_key, (), 0, groups).astype(jnp.int32)
    lengths = jnp.where(jnp.arange(groups, dtype=jnp.int32) == chosen, TOK_DEV, lengths)
    offsets = jnp.arange(TOK_DEV, dtype=jnp.int32)
    livemask = (offsets[None, :] < lengths[:, None]).astype(jnp.int32)
    return livemask.reshape(TOKENS)


def draw_inputs(key, part):
    groups = TOKENS // TOK_DEV
    base = jax.random.fold_in(key, 31)
    drawn_key = jax.random.fold_in(base, 0)
    values = jnp.clip(jax.random.normal(drawn_key, (groups, TOK_DEV, D), jnp.float32), -6.0, 6.0)
    return values.reshape(TOKENS, D).astype(jnp.bfloat16)


def draw_triple_weight(key, part):
    base = jax.random.fold_in(key, 23)
    query_key, other_key, value_key = jax.random.split(base, 3)
    query_block = jnp.clip(jax.random.normal(query_key, (D, D), jnp.float32), -6.0, 6.0)
    other_block = jnp.clip(jax.random.normal(other_key, (D, D), jnp.float32), -6.0, 6.0)
    value_block = jnp.clip(jax.random.normal(value_key, (D, D), jnp.float32), -6.0, 6.0)
    key_block = other_block
    whole = jnp.concatenate([query_block, key_block, value_block], axis=1) * D ** (-0.5)
    return whole.astype(jnp.bfloat16)


def strengthened(values, key, source, target, blocks, factor):
    def block_of(position):
        return (jnp.arange(values.shape[position]) // (values.shape[position] // blocks)).reshape((-1,) + (1,) * (values.ndim - 1 - position))

    near = jax.random.permutation(key, blocks)[block_of(target)]
    far = (block_of(target) + blocks // 2) % blocks
    return jnp.where((block_of(source) == near) | (block_of(source) == far), factor * values, values)


def shard_levels(own_key, dims, shards, smallest, largest):
    def one(dim, parts):
        draws = jax.random.uniform(jax.random.fold_in(jax.random.fold_in(own_key, 6), dim), (parts,), jnp.float32, smallest / len(shards), largest / len(shards))
        return jnp.repeat(jnp.exp(draws), dims[dim] // parts).reshape((-1,) + (1,) * (len(dims) - dim - 1))

    factor_of = one(*shards[0])
    for cut in shards[1:]:
        factor_of = factor_of * one(*cut)
    return factor_of


def normal_values(rng, dims, spread, most, shards=(), kind=jnp.bfloat16):
    values = jax.random.normal(rng, dims, jnp.float32) * spread
    if len(shards) > 0:
        values = shard_levels(rng, dims, shards, -0.22, 0.18) * values
    return jnp.clip(values, min=-most, max=most).astype(kind)


def bell_draw_with(stream_key, extent, scale, most, cuts, heavy, kind=jnp.bfloat16):
    values = scale * jax.random.normal(stream_key, extent, jnp.float32)
    if cuts:
        values = values * shard_levels(stream_key, extent, cuts, -0.22, 0.18)
    return jnp.clip(strengthened(values, jax.random.fold_in(stream_key, 3), *heavy), -most, most).astype(kind)


def setup_inputs(seed: int = 0) -> dict:
    key_of = jax.random.split(jax.random.key(seed), 17)
    inputs = draw_inputs(jax.random.fold_in(key_of[16], 71), 0)
    live_keys = draw_live_keys(jax.random.fold_in(key_of[16], 71), 0)
    triple_weight = draw_triple_weight(jax.random.fold_in(key_of[16], 71), 0)
    query_bias = normal_values(key_of[3], (D,), 0.5, 3.0, ((0, 32),))
    value_bias = normal_values(key_of[4], (D,), 0.5, 3.0, ((0, 32),))
    output_weight = normal_values(key_of[5], (D, D), (D // 64) ** -0.5, 1.5, ((0, 32),))
    output_bias = normal_values(key_of[6], (D,), 0.5, 3.0, ((0, 32),))
    first_gain = jnp.clip(1.0 + 0.1 * jax.random.normal(key_of[7], (D,), jnp.float32), 0.5, 1.5).astype(jnp.bfloat16)
    first_shift = normal_values(key_of[8], (D,), 0.5, 3.0, ((0, 32),))
    expand_weight = normal_values(key_of[9], (D, FF), D ** -0.5, 0.1875, ((0, 32),))
    expand_bias = normal_values(key_of[10], (FF,), 0.5, 3.0, ((0, 32),))
    shrink_weight = normal_values(key_of[11], (FF, D), FF ** -0.5, 0.09375, ((0, 32),))
    shrink_bias = normal_values(key_of[12], (D,), 0.5, 3.0, ((0, 32),))
    second_gain = jnp.clip(1.0 + 0.1 * jax.random.normal(key_of[13], (D,), jnp.float32), 0.5, 1.5).astype(jnp.bfloat16)
    second_shift = normal_values(key_of[14], (D,), 0.5, 3.0, ((0, 32),))
    cotangent = bell_draw_with(key_of[15], (TOKENS, D), 1.0, 6.0, ((0, 32),), (0, 1, 32, 2.75))
    return {"inputs": inputs, "live_keys": live_keys, "triple_weight": triple_weight, "query_bias": query_bias, "value_bias": value_bias, "output_weight": output_weight, "output_bias": output_bias, "first_gain": first_gain, "first_shift": first_shift, "expand_weight": expand_weight, "expand_bias": expand_bias, "shrink_weight": shrink_weight, "shrink_bias": shrink_bias, "second_gain": second_gain, "second_shift": second_shift, "cotangent": cotangent}


EPSILON = 1e-05
NEGATIVE = -1e+30
ROOT_HALF = 0.7071067811865476
INV_ROOT_TWO_PI = 0.3989422804014327

def batched(form, left, right):
    return jnp.einsum(form, left.astype(jnp.float32), right.astype(jnp.float32))

def layer_norm(hidden, gain, shift):
    center = hidden - lax.optimization_barrier(jnp.mean(hidden, axis=-1, keepdims=True))
    inv_std = lax.rsqrt(lax.optimization_barrier(jnp.mean(center * center, axis=-1, keepdims=True)) + EPSILON)
    normed = center * inv_std
    return (normed * gain.astype(jnp.float32) + shift.astype(jnp.float32), normed, inv_std)

def layer_norm_back(upstream, normed, inv_std, gain):
    scaled = upstream * gain.astype(jnp.float32)
    inner = scaled - lax.optimization_barrier(jnp.mean(scaled, axis=-1, keepdims=True)) - normed * lax.optimization_barrier(jnp.mean(scaled * normed, axis=-1, keepdims=True))
    return (inv_std * inner, lax.optimization_barrier(jnp.sum(upstream * normed, axis=0)), lax.optimization_barrier(jnp.sum(upstream, axis=0)))

def normal_cdf(values):
    return 0.5 * (1.0 + lax.erf(values * ROOT_HALF))

def masked_scores(query, keys, live):
    scores = batched('qhd,khd->hqk', query, keys)
    allowed = live == 1
    return jnp.where(allowed[None, None, :], scores, NEGATIVE)

def forward(params, tokens, live):
    triple_weight, query_bias, value_bias, output_weight, output_bias, first_gain, first_shift, expand_weight, expand_bias, shrink_weight, shrink_bias, second_gain, second_shift = params
    row_count = tokens.shape[0]
    width_all = tokens.shape[1]
    head_size = width_all // HEADS
    factor = head_size ** (-0.5)
    projected = jnp.dot(tokens, triple_weight, preferred_element_type=jnp.float32)
    query = ((projected[:, :width_all] + query_bias.astype(jnp.float32)) * factor).astype(jnp.bfloat16)
    keys = projected[:, width_all:2 * width_all].astype(jnp.bfloat16)
    values = (projected[:, 2 * width_all:] + value_bias.astype(jnp.float32)).astype(jnp.bfloat16)
    query = query.reshape(row_count, HEADS, head_size)
    keys = keys.reshape(row_count, HEADS, head_size)
    values = values.reshape(row_count, HEADS, head_size)
    scores = masked_scores(query, keys, live)
    top = lax.optimization_barrier(jnp.max(scores, axis=-1, keepdims=True))
    expo = jnp.exp(scores - top)
    total = lax.optimization_barrier(jnp.sum(expo, axis=-1, keepdims=True))
    log_total = top + jnp.log(total)
    probs = (expo / total).astype(jnp.bfloat16)
    context = batched('hqk,khd->qhd', probs, values).astype(jnp.bfloat16).reshape(row_count, width_all)
    first_in = tokens.astype(jnp.float32) + jnp.dot(context, output_weight, preferred_element_type=jnp.float32) + output_bias.astype(jnp.float32)
    middle, first_norm, first_rate = layer_norm(first_in, first_gain, first_shift)
    mid_low = middle.astype(jnp.bfloat16)
    pre_act = jnp.dot(mid_low, expand_weight, preferred_element_type=jnp.float32) + expand_bias.astype(jnp.float32)
    act_low = (pre_act * normal_cdf(pre_act)).astype(jnp.bfloat16)
    second_in = middle + jnp.dot(act_low, shrink_weight, preferred_element_type=jnp.float32) + shrink_bias.astype(jnp.float32)
    result, second_norm, second_rate = layer_norm(second_in, second_gain, second_shift)
    saved = (tokens, live, query, keys, values, log_total, context, first_norm, first_rate, mid_low, pre_act, act_low, second_norm, second_rate)
    return (result.astype(jnp.bfloat16), saved)

def back_upper(params, saved, upstream):
    triple_weight, query_bias, value_bias, output_weight, output_bias, first_gain, first_shift, expand_weight, expand_bias, shrink_weight, shrink_bias, second_gain, second_shift = params
    tokens, live, query, keys, values, log_total, context, first_norm, first_rate, mid_low, pre_act, act_low, second_norm, second_rate = saved
    d_second, second_gain_grad, second_shift_grad = layer_norm_back(upstream.astype(jnp.float32), second_norm, second_rate, second_gain)
    d_second_low = d_second.astype(jnp.bfloat16)
    shrink_grad = jnp.dot(act_low.T, d_second_low, preferred_element_type=jnp.float32)
    shrink_bias_grad = lax.optimization_barrier(jnp.sum(d_second, axis=0))
    d_act = jnp.dot(d_second_low, shrink_weight.T, preferred_element_type=jnp.float32)
    slope = normal_cdf(pre_act) + pre_act * jnp.exp(-0.5 * pre_act * pre_act) * INV_ROOT_TWO_PI
    d_pre = d_act * slope
    expand_bias_grad = lax.optimization_barrier(jnp.sum(d_pre, axis=0))
    d_pre_low = d_pre.astype(jnp.bfloat16)
    expand_grad = jnp.dot(mid_low.T, d_pre_low, preferred_element_type=jnp.float32)
    d_mid = d_second + jnp.dot(d_pre_low, expand_weight.T, preferred_element_type=jnp.float32)
    d_first, first_gain_grad, first_shift_grad = layer_norm_back(d_mid, first_norm, first_rate, first_gain)
    grads = (first_gain_grad, first_shift_grad, expand_grad, expand_bias_grad, shrink_grad, shrink_bias_grad, second_gain_grad, second_shift_grad)
    return (grads, d_first)

def back_lower(params, saved, d_first):
    triple_weight, query_bias, value_bias, output_weight, output_bias, first_gain, first_shift, expand_weight, expand_bias, shrink_weight, shrink_bias, second_gain, second_shift = params
    tokens, live, query, keys, values, log_total, context, first_norm, first_rate, mid_low, pre_act, act_low, second_norm, second_rate = saved
    row_count = tokens.shape[0]
    width_all = tokens.shape[1]
    head_size = width_all // HEADS
    factor = head_size ** (-0.5)
    d_first_low = d_first.astype(jnp.bfloat16)
    output_grad = jnp.dot(context.T, d_first_low, preferred_element_type=jnp.float32)
    output_bias_grad = lax.optimization_barrier(jnp.sum(d_first, axis=0))
    d_context = jnp.dot(d_first_low, output_weight.T, preferred_element_type=jnp.float32).astype(jnp.bfloat16)
    d_context = d_context.reshape(row_count, HEADS, head_size)
    scores = masked_scores(query, keys, live)
    probs = jnp.exp(scores - log_total)
    probs_low = probs.astype(jnp.bfloat16)
    d_values = batched('hqk,qhd->khd', probs_low, d_context)
    d_probs = batched('qhd,khd->hqk', d_context, values)
    inner = lax.optimization_barrier(jnp.sum(probs * d_probs, axis=-1, keepdims=True))
    d_scores = (probs * (d_probs - inner)).astype(jnp.bfloat16)
    d_query = factor * batched('hqk,khd->qhd', d_scores, keys)
    d_keys = batched('hqk,qhd->khd', d_scores, query)
    d_query = d_query.reshape(row_count, width_all)
    d_keys = d_keys.reshape(row_count, width_all)
    d_values = d_values.reshape(row_count, width_all)
    d_proj = jnp.concatenate([d_query, d_keys, d_values], axis=1).astype(jnp.bfloat16)
    triple_grad = jnp.dot(tokens.T, d_proj, preferred_element_type=jnp.float32)
    query_bias_grad = lax.optimization_barrier(jnp.sum(d_query, axis=0))
    value_bias_grad = lax.optimization_barrier(jnp.sum(d_values, axis=0))
    input_grad = (d_first + jnp.dot(d_proj, triple_weight.T, preferred_element_type=jnp.float32)).astype(jnp.bfloat16)
    grads = (triple_grad, query_bias_grad, value_bias_grad, output_grad, output_bias_grad)
    return (grads, input_grad)

def reference(inputs, live_keys, triple_weight, query_bias, value_bias, output_weight, output_bias, first_gain, first_shift, expand_weight, expand_bias, shrink_weight, shrink_bias, second_gain, second_shift, cotangent):
    params = (triple_weight, query_bias, value_bias, output_weight, output_bias, first_gain, first_shift, expand_weight, expand_bias, shrink_weight, shrink_bias, second_gain, second_shift)
    groups = TOKENS // TOK_DEV
    series = (inputs.reshape(groups, TOK_DEV, D), live_keys.reshape(groups, TOK_DEV), cotangent.reshape(groups, TOK_DEV, D))
    zeros = tuple((jnp.zeros(item.shape, jnp.float32) for item in params))

    def advance(carry, element):
        tokens, live, upstream = element
        result, saved = forward(params, tokens, live)
        upper, d_first = back_upper(params, saved, upstream)
        lower, input_grad = back_lower(params, saved, d_first)
        grads = lower + upper
        return (tuple((old + new for old, new in zip(carry, grads))), (result, input_grad))
    totals, (results, input_grads) = lax.scan(advance, zeros, series)
    return (results.reshape(TOKENS, D), input_grads.reshape(TOKENS, D), totals[0], totals[1], totals[2], totals[3], totals[4], totals[5], totals[6], totals[7], totals[8], totals[9], totals[10], totals[11], totals[12])
```

```python
import jax
import jax.numpy as jnp
from jax import lax
from jax.sharding import PartitionSpec as P

HEADS = 16


EPSILON = 1e-05
NEGATIVE = -1e30
ROOT_HALF = 0.7071067811865476
INV_ROOT_TWO_PI = 0.3989422804014327


def batched(form, left, right):
    return jnp.einsum(form, left, right, preferred_element_type=jnp.float32)


def layer_norm(hidden, gain, shift):
    center = hidden - jnp.mean(hidden, axis=-1, keepdims=True)
    inv_std = lax.rsqrt(jnp.mean(center * center, axis=-1, keepdims=True) + EPSILON)
    normed = center * inv_std
    return (normed * gain.astype(jnp.float32) + shift.astype(jnp.float32), normed, inv_std)


def layer_norm_back(upstream, normed, inv_std, gain):
    scaled = upstream * gain.astype(jnp.float32)
    inner = (
        scaled
        - jnp.mean(scaled, axis=-1, keepdims=True)
        - normed * jnp.mean(scaled * normed, axis=-1, keepdims=True)
    )
    return (inv_std * inner, jnp.sum(upstream * normed, axis=0), jnp.sum(upstream, axis=0))


def normal_cdf(values):
    return 0.5 * (1.0 + lax.erf(values * ROOT_HALF))


def masked_scores(query, keys, live):
    scores = batched("qhd,khd->hqk", query, keys)
    allowed = live == 1
    return jnp.where(allowed[None, None, :], scores, NEGATIVE)


def forward(params, tokens, live):
    (
        triple_weight,
        query_bias,
        value_bias,
        output_weight,
        output_bias,
        first_gain,
        first_shift,
        expand_weight,
        expand_bias,
        shrink_weight,
        shrink_bias,
        second_gain,
        second_shift,
    ) = params
    row_count = tokens.shape[0]
    width_all = tokens.shape[1]
    head_size = width_all // HEADS
    factor = head_size ** (-0.5)
    projected = jnp.dot(tokens, triple_weight, preferred_element_type=jnp.float32)
    query = ((projected[:, :width_all] + query_bias.astype(jnp.float32)) * factor).astype(
        jnp.bfloat16
    )
    keys = projected[:, width_all : 2 * width_all].astype(jnp.bfloat16)
    values = (projected[:, 2 * width_all :] + value_bias.astype(jnp.float32)).astype(jnp.bfloat16)
    query = query.reshape(row_count, HEADS, head_size)
    keys = keys.reshape(row_count, HEADS, head_size)
    values = values.reshape(row_count, HEADS, head_size)
    scores = masked_scores(query, keys, live)
    top = jnp.max(scores, axis=-1, keepdims=True)
    expo = jnp.exp(scores - top)
    total = jnp.sum(expo, axis=-1, keepdims=True)
    log_total = top + jnp.log(total)
    probs = (expo / total).astype(jnp.bfloat16)
    context = (
        batched("hqk,khd->qhd", probs, values).astype(jnp.bfloat16).reshape(row_count, width_all)
    )
    first_in = (
        tokens.astype(jnp.float32)
        + jnp.dot(context, output_weight, preferred_element_type=jnp.float32)
        + output_bias.astype(jnp.float32)
    )
    middle, first_norm, first_rate = layer_norm(first_in, first_gain, first_shift)
    mid_low = middle.astype(jnp.bfloat16)
    pre_act = jnp.dot(
        mid_low, expand_weight, preferred_element_type=jnp.float32
    ) + expand_bias.astype(jnp.float32)
    act_low = (pre_act * normal_cdf(pre_act)).astype(jnp.bfloat16)
    second_in = (
        middle
        + jnp.dot(act_low, shrink_weight, preferred_element_type=jnp.float32)
        + shrink_bias.astype(jnp.float32)
    )
    result, second_norm, second_rate = layer_norm(second_in, second_gain, second_shift)
    saved = (
        tokens,
        live,
        query,
        keys,
        values,
        log_total,
        context,
        first_norm,
        first_rate,
        mid_low,
        pre_act,
        act_low,
        second_norm,
        second_rate,
    )
    return (result.astype(jnp.bfloat16), saved)


def back_upper(params, saved, upstream):
    (
        triple_weight,
        query_bias,
        value_bias,
        output_weight,
        output_bias,
        first_gain,
        first_shift,
        expand_weight,
        expand_bias,
        shrink_weight,
        shrink_bias,
        second_gain,
        second_shift,
    ) = params
    (
        tokens,
        live,
        query,
        keys,
        values,
        log_total,
        context,
        first_norm,
        first_rate,
        mid_low,
        pre_act,
        act_low,
        second_norm,
        second_rate,
    ) = saved
    d_second, second_gain_grad, second_shift_grad = layer_norm_back(
        upstream.astype(jnp.float32), second_norm, second_rate, second_gain
    )
    d_second_low = d_second.astype(jnp.bfloat16)
    shrink_bias_grad = jnp.sum(d_second, axis=0)
    d_act = jnp.dot(d_second_low, shrink_weight.T, preferred_element_type=jnp.float32)
    slope = normal_cdf(pre_act) + pre_act * jnp.exp(-0.5 * pre_act * pre_act) * INV_ROOT_TWO_PI
    d_pre = d_act * slope
    expand_bias_grad = jnp.sum(d_pre, axis=0)
    d_pre_low = d_pre.astype(jnp.bfloat16)
    d_mid = d_second + jnp.dot(d_pre_low, expand_weight.T, preferred_element_type=jnp.float32)
    d_first, first_gain_grad, first_shift_grad = layer_norm_back(
        d_mid, first_norm, first_rate, first_gain
    )
    small = (
        first_gain_grad,
        first_shift_grad,
        expand_bias_grad,
        shrink_bias_grad,
        second_gain_grad,
        second_shift_grad,
    )
    pairs = ((mid_low, d_pre_low), (act_low, d_second_low))
    return (small, pairs, d_first)


def back_lower(params, saved, d_first):
    (
        triple_weight,
        query_bias,
        value_bias,
        output_weight,
        output_bias,
        first_gain,
        first_shift,
        expand_weight,
        expand_bias,
        shrink_weight,
        shrink_bias,
        second_gain,
        second_shift,
    ) = params
    (
        tokens,
        live,
        query,
        keys,
        values,
        log_total,
        context,
        first_norm,
        first_rate,
        mid_low,
        pre_act,
        act_low,
        second_norm,
        second_rate,
    ) = saved
    row_count = tokens.shape[0]
    width_all = tokens.shape[1]
    head_size = width_all // HEADS
    factor = head_size ** (-0.5)
    d_first_low = d_first.astype(jnp.bfloat16)
    output_bias_grad = jnp.sum(d_first, axis=0)
    d_context = jnp.dot(d_first_low, output_weight.T, preferred_element_type=jnp.float32).astype(
        jnp.bfloat16
    )
    d_context = d_context.reshape(row_count, HEADS, head_size)
    scores = masked_scores(query, keys, live)
    probs = jnp.exp(scores - log_total)
    probs_low = probs.astype(jnp.bfloat16)
    d_values = batched("hqk,qhd->khd", probs_low, d_context)
    d_probs = batched("qhd,khd->hqk", d_context, values)
    inner = jnp.sum(probs * d_probs, axis=-1, keepdims=True)
    d_scores = (probs * (d_probs - inner)).astype(jnp.bfloat16)
    d_query = factor * batched("hqk,khd->qhd", d_scores, keys)
    d_keys = batched("hqk,qhd->khd", d_scores, query)
    d_query = d_query.reshape(row_count, width_all)
    d_keys = d_keys.reshape(row_count, width_all)
    d_values = d_values.reshape(row_count, width_all)
    d_proj = jnp.concatenate([d_query, d_keys, d_values], axis=1).astype(jnp.bfloat16)
    query_bias_grad = jnp.sum(d_query, axis=0)
    value_bias_grad = jnp.sum(d_values, axis=0)
    input_grad = (
        d_first + jnp.dot(d_proj, triple_weight.T, preferred_element_type=jnp.float32)
    ).astype(jnp.bfloat16)
    small = (query_bias_grad, value_bias_grad, output_bias_grad)
    pairs = ((tokens, d_proj), (context, d_first_low))
    return (small, pairs, input_grad)


def swap(value, bit, count):
    return lax.ppermute(value, "fsdp", [(i, i ^ (1 << bit)) for i in range(count)])


def own_bit(bit):
    return (lax.axis_index("fsdp") >> bit) & 1


def join(own, other, bit, levels):
    first = own_bit(bit) == 0
    return jnp.concatenate(
        [jnp.where(first, own, other), jnp.where(first, other, own)], axis=levels - 1 - bit
    )


def orders(levels):
    ring = list(range(1, levels))
    return [ring[k * len(ring) // 3 :] + ring[: k * len(ring) // 3] for k in range(3)]


def collect(shard, order, count):
    levels = count.bit_length() - 1
    held = shard.reshape((1,) * levels + shard.shape)
    steps = list(reversed(order))
    for bit in steps[:-1]:
        held = join(held, swap(held, bit, count), bit, levels)
    bit = steps[-1]
    across = swap(held, bit, count)
    beside = swap(held, 0, count)
    corner = swap(across, 0, count)
    held = join(join(held, across, bit, levels), join(beside, corner, bit, levels), 0, levels)
    return held.reshape((count * shard.shape[0],) + shard.shape[1:])


def halve(terms, order, count, last):
    levels = count.bit_length() - 1
    for bit in order:
        axis = terms.ndim - 3 - bit if last else terms.ndim - 2 - bit
        mine = own_bit(bit)
        keep = lax.dynamic_slice_in_dim(terms, mine, 1, axis)
        send = lax.dynamic_slice_in_dim(terms, 1 - mine, 1, axis)
        total = keep.astype(jnp.float32) + swap(send, bit, count).astype(jnp.float32)
        terms = total if bit == order[-1] else total.astype(terms.dtype)
    return terms.reshape(terms.shape[-2:])


def by_core(left, count):
    parts = left.reshape(left.shape[0], count // 2, 2, left.shape[1] // count)
    core = own_bit(0)
    pick = lambda at: lax.dynamic_index_in_dim(parts, at, 2, keepdims=False).reshape(
        left.shape[0], left.shape[1] // 2
    )
    return (pick(core), pick(1 - core))


def pair_up(left, right, count):
    mine, other = by_core(left, count)
    return (
        jnp.concatenate([mine, swap(other, 0, count)], axis=0),
        jnp.concatenate([right, swap(right, 0, count)], axis=0),
    )


def summed_grad(left, right, pieces, count):
    levels = count.bit_length() - 1
    results = []
    offset = 0
    for extent, order in pieces:
        term = jnp.einsum(
            "tk,tw->kw",
            left,
            right[:, offset : offset + extent],
            preferred_element_type=jnp.float32,
        ).astype(jnp.bfloat16)
        term = term.reshape((2,) * (levels - 1) + (left.shape[1] * 2 // count, extent))
        results.append(halve(term, order, count, False))
        offset = offset + extent
    return results[0] if len(results) == 1 else jnp.concatenate(results, axis=1)


def body(
    inputs,
    live_keys,
    triple_weight,
    query_bias,
    value_bias,
    output_weight,
    output_bias,
    first_gain,
    first_shift,
    expand_weight,
    expand_bias,
    shrink_weight,
    shrink_bias,
    second_gain,
    second_shift,
    cotangent,
):
    count = lax.axis_size("fsdp")
    levels = count.bit_length() - 1
    width = inputs.shape[1]
    ways = orders(levels)
    vectors = (
        query_bias,
        value_bias,
        output_bias,
        first_gain,
        first_shift,
        expand_bias,
        shrink_bias,
        second_gain,
        second_shift,
    )
    packed = collect(jnp.concatenate(vectors)[None, :], ways[0], count)
    wide = []
    offset = 0
    for vector in vectors:
        wide.append(packed[:, offset : offset + vector.shape[0]].reshape(-1))
        offset = offset + vector.shape[0]
    gathered = (
        collect(triple_weight, ways[2], count),
        wide[0],
        wide[1],
        collect(output_weight, ways[0], count),
        wide[2],
        wide[3],
        wide[4],
        collect(expand_weight, ways[0], count),
        wide[5],
        collect(shrink_weight, ways[1], count),
        wide[6],
        wide[7],
        wide[8],
    )
    layer_out, saved = forward(gathered, inputs, live_keys)
    upper_small, upper_pairs, d_first = back_upper(gathered, saved, cotangent)
    lower_small, lower_pairs, input_grad = back_lower(gathered, saved, d_first)
    hidden = expand_weight.shape[1]
    shrink_grad = summed_grad(
        *pair_up(*upper_pairs[1], count),
        ((width * 3 // 4, ways[1]), (width // 4, ways[2])),
        count,
    )
    expand_grad = summed_grad(
        *pair_up(*upper_pairs[0], count),
        ((hidden * 3 // 4, ways[0]), (hidden // 4, ways[2])),
        count,
    )
    output_grad = summed_grad(*pair_up(*lower_pairs[1], count), ((width, ways[1]),), count)
    triple_grad = summed_grad(
        *pair_up(*lower_pairs[0], count),
        ((width, ways[0]), (width, ways[1]), (width, ways[2])),
        count,
    )
    sums = lower_small + upper_small
    terms = jnp.concatenate([item.reshape(count, -1) for item in sums], axis=1)
    terms = terms.reshape((2,) * levels + (1, terms.shape[1]))
    owned = halve(terms, list(range(levels)), count, True)[0]
    small = []
    offset = 0
    for item in sums:
        extent = item.shape[0] // count
        small.append(owned[offset : offset + extent])
        offset = offset + extent
    return (
        layer_out,
        input_grad,
        triple_grad,
        small[0],
        small[1],
        output_grad,
        small[2],
        small[3],
        small[4],
        expand_grad,
        small[5],
        shrink_grad,
        small[6],
        small[7],
        small[8],
    )


def solution(mesh):
    placed = (
        P("fsdp", None),
        P("fsdp"),
        P("fsdp", None),
        P("fsdp"),
        P("fsdp"),
        P("fsdp", None),
        P("fsdp"),
        P("fsdp"),
        P("fsdp"),
        P("fsdp", None),
        P("fsdp"),
        P("fsdp", None),
        P("fsdp"),
        P("fsdp"),
        P("fsdp"),
        P("fsdp", None),
    )
    return jax.shard_map(
        body,
        mesh=mesh,
        in_specs=placed,
        out_specs=(
            P("fsdp", None),
            P("fsdp", None),
            P("fsdp", None),
            P("fsdp"),
            P("fsdp"),
            P("fsdp", None),
            P("fsdp"),
            P("fsdp"),
            P("fsdp"),
            P("fsdp", None),
            P("fsdp"),
            P("fsdp", None),
            P("fsdp"),
            P("fsdp"),
            P("fsdp"),
        ),
        check_vma=False,
    )
```

```python
import jax
import jax.numpy as jnp
from jax import lax
from jax.sharding import PartitionSpec as P

HEADS = 16


EPSILON = 1e-05
NEGATIVE = -1e30
ROOT_HALF = 0.7071067811865476
INV_ROOT_TWO_PI = 0.3989422804014327


def batched(form, left, right):
    return jnp.einsum(form, left, right, preferred_element_type=jnp.float32)


def layer_norm(hidden, gain, shift):
    center = hidden - jnp.mean(hidden, axis=-1, keepdims=True)
    inv_std = lax.rsqrt(jnp.mean(center * center, axis=-1, keepdims=True) + EPSILON)
    normed = center * inv_std
    return (normed * gain.astype(jnp.float32) + shift.astype(jnp.float32), normed, inv_std)


def layer_norm_back(upstream, normed, inv_std, gain):
    scaled = upstream * gain.astype(jnp.float32)
    inner = (
        scaled
        - jnp.mean(scaled, axis=-1, keepdims=True)
        - normed * jnp.mean(scaled * normed, axis=-1, keepdims=True)
    )
    return (inv_std * inner, jnp.sum(upstream * normed, axis=0), jnp.sum(upstream, axis=0))


def normal_cdf(values):
    return 0.5 * (1.0 + lax.erf(values * ROOT_HALF))


def masked_scores(query, keys, live):
    scores = batched("qhd,khd->hqk", query, keys)
    allowed = live == 1
    return jnp.where(allowed[None, None, :], scores, NEGATIVE)


def forward(params, tokens, live):
    (
        triple_weight,
        query_bias,
        value_bias,
        output_weight,
        output_bias,
        first_gain,
        first_shift,
        expand_weight,
        expand_bias,
        shrink_weight,
        shrink_bias,
        second_gain,
        second_shift,
    ) = params
    row_count = tokens.shape[0]
    width_all = tokens.shape[1]
    head_size = width_all // HEADS
    factor = head_size ** (-0.5)
    projected = jnp.dot(tokens, triple_weight, preferred_element_type=jnp.float32)
    query = ((projected[:, :width_all] + query_bias.astype(jnp.float32)) * factor).astype(
        jnp.bfloat16
    )
    keys = projected[:, width_all : 2 * width_all].astype(jnp.bfloat16)
    values = (projected[:, 2 * width_all :] + value_bias.astype(jnp.float32)).astype(jnp.bfloat16)
    query = query.reshape(row_count, HEADS, head_size)
    keys = keys.reshape(row_count, HEADS, head_size)
    values = values.reshape(row_count, HEADS, head_size)
    scores = masked_scores(query, keys, live)
    top = jnp.max(scores, axis=-1, keepdims=True)
    expo = jnp.exp(scores - top)
    total = jnp.sum(expo, axis=-1, keepdims=True)
    log_total = top + jnp.log(total)
    probs = (expo / total).astype(jnp.bfloat16)
    context = (
        batched("hqk,khd->qhd", probs, values).astype(jnp.bfloat16).reshape(row_count, width_all)
    )
    first_in = (
        tokens.astype(jnp.float32)
        + jnp.dot(context, output_weight, preferred_element_type=jnp.float32)
        + output_bias.astype(jnp.float32)
    )
    middle, first_norm, first_rate = layer_norm(first_in, first_gain, first_shift)
    mid_low = middle.astype(jnp.bfloat16)
    pre_act = jnp.dot(
        mid_low, expand_weight, preferred_element_type=jnp.float32
    ) + expand_bias.astype(jnp.float32)
    act_low = (pre_act * normal_cdf(pre_act)).astype(jnp.bfloat16)
    second_in = (
        middle
        + jnp.dot(act_low, shrink_weight, preferred_element_type=jnp.float32)
        + shrink_bias.astype(jnp.float32)
    )
    result, second_norm, second_rate = layer_norm(second_in, second_gain, second_shift)
    saved = (
        tokens,
        live,
        query,
        keys,
        values,
        log_total,
        context,
        first_norm,
        first_rate,
        mid_low,
        pre_act,
        act_low,
        second_norm,
        second_rate,
    )
    return (result.astype(jnp.bfloat16), saved)


def back_upper(params, saved, upstream):
    (
        triple_weight,
        query_bias,
        value_bias,
        output_weight,
        output_bias,
        first_gain,
        first_shift,
        expand_weight,
        expand_bias,
        shrink_weight,
        shrink_bias,
        second_gain,
        second_shift,
    ) = params
    (
        tokens,
        live,
        query,
        keys,
        values,
        log_total,
        context,
        first_norm,
        first_rate,
        mid_low,
        pre_act,
        act_low,
        second_norm,
        second_rate,
    ) = saved
    d_second, second_gain_grad, second_shift_grad = layer_norm_back(
        upstream.astype(jnp.float32), second_norm, second_rate, second_gain
    )
    d_second_low = d_second.astype(jnp.bfloat16)
    shrink_bias_grad = jnp.sum(d_second, axis=0)
    d_act = jnp.dot(d_second_low, shrink_weight.T, preferred_element_type=jnp.float32)
    slope = normal_cdf(pre_act) + pre_act * jnp.exp(-0.5 * pre_act * pre_act) * INV_ROOT_TWO_PI
    d_pre = d_act * slope
    expand_bias_grad = jnp.sum(d_pre, axis=0)
    d_pre_low = d_pre.astype(jnp.bfloat16)
    d_mid = d_second + jnp.dot(d_pre_low, expand_weight.T, preferred_element_type=jnp.float32)
    d_first, first_gain_grad, first_shift_grad = layer_norm_back(
        d_mid, first_norm, first_rate, first_gain
    )
    small = (
        first_gain_grad,
        first_shift_grad,
        expand_bias_grad,
        shrink_bias_grad,
        second_gain_grad,
        second_shift_grad,
    )
    pairs = ((mid_low, d_pre_low), (act_low, d_second_low))
    return (small, pairs, d_first)


def back_lower(params, saved, d_first):
    (
        triple_weight,
        query_bias,
        value_bias,
        output_weight,
        output_bias,
        first_gain,
        first_shift,
        expand_weight,
        expand_bias,
        shrink_weight,
        shrink_bias,
        second_gain,
        second_shift,
    ) = params
    (
        tokens,
        live,
        query,
        keys,
        values,
        log_total,
        context,
        first_norm,
        first_rate,
        mid_low,
        pre_act,
        act_low,
        second_norm,
        second_rate,
    ) = saved
    row_count = tokens.shape[0]
    width_all = tokens.shape[1]
    head_size = width_all // HEADS
    factor = head_size ** (-0.5)
    d_first_low = d_first.astype(jnp.bfloat16)
    output_bias_grad = jnp.sum(d_first, axis=0)
    d_context = jnp.dot(d_first_low, output_weight.T, preferred_element_type=jnp.float32).astype(
        jnp.bfloat16
    )
    d_context = d_context.reshape(row_count, HEADS, head_size)
    scores = masked_scores(query, keys, live)
    probs = jnp.exp(scores - log_total)
    probs_low = probs.astype(jnp.bfloat16)
    d_values = batched("hqk,qhd->khd", probs_low, d_context)
    d_probs = batched("qhd,khd->hqk", d_context, values)
    inner = jnp.sum(probs * d_probs, axis=-1, keepdims=True)
    d_scores = (probs * (d_probs - inner)).astype(jnp.bfloat16)
    d_query = factor * batched("hqk,khd->qhd", d_scores, keys)
    d_keys = batched("hqk,qhd->khd", d_scores, query)
    d_query = d_query.reshape(row_count, width_all)
    d_keys = d_keys.reshape(row_count, width_all)
    d_values = d_values.reshape(row_count, width_all)
    d_proj = jnp.concatenate([d_query, d_keys, d_values], axis=1).astype(jnp.bfloat16)
    query_bias_grad = jnp.sum(d_query, axis=0)
    value_bias_grad = jnp.sum(d_values, axis=0)
    input_grad = (
        d_first + jnp.dot(d_proj, triple_weight.T, preferred_element_type=jnp.float32)
    ).astype(jnp.bfloat16)
    small = (query_bias_grad, value_bias_grad, output_bias_grad)
    pairs = ((tokens, d_proj), (context, d_first_low))
    return (small, pairs, input_grad)


def swap(value, bit, count):
    return lax.ppermute(value, "fsdp", [(i, i ^ (1 << bit)) for i in range(count)])


def own_bit(bit):
    return (lax.axis_index("fsdp") >> bit) & 1


def place(base, value, places, levels):
    starts = [0] * base.ndim
    for bit, at in places:
        starts[levels - 1 - bit] = at
    return lax.dynamic_update_slice(base, value, starts)


def grown(value, bits, levels):
    shape = list(value.shape)
    for bit in bits:
        shape[levels - 1 - bit] = 2
    return jnp.zeros(shape, value.dtype)


def join(own, other, bit, levels):
    mine = own_bit(bit)
    base = place(grown(own, (bit,), levels), own, ((bit, mine),), levels)
    return place(base, other, ((bit, 1 - mine),), levels)


def orders(levels):
    ring = list(range(1, levels))
    return [ring[k * len(ring) // 3 :] + ring[: k * len(ring) // 3] for k in range(3)]


def collect(shard, order, count):
    levels = count.bit_length() - 1
    held = shard.reshape((1,) * levels + shard.shape)
    steps = list(reversed(order))
    for bit in steps[:-1]:
        held = join(held, swap(held, bit, count), bit, levels)
    bit = steps[-1]
    across = swap(held, bit, count)
    beside = swap(held, 0, count)
    corner = swap(across, 0, count)
    mine, core = own_bit(bit), own_bit(0)
    full = grown(held, (bit, 0), levels)
    full = place(full, held, ((bit, mine), (0, core)), levels)
    full = place(full, beside, ((bit, mine), (0, 1 - core)), levels)
    full = place(full, across, ((bit, 1 - mine), (0, core)), levels)
    held = place(full, corner, ((bit, 1 - mine), (0, 1 - core)), levels)
    return held.reshape((count * shard.shape[0],) + shard.shape[1:])


def halve(terms, order, count, last):
    levels = count.bit_length() - 1
    for bit in order:
        axis = terms.ndim - 3 - bit if last else terms.ndim - 2 - bit
        mine = own_bit(bit)
        keep = lax.dynamic_slice_in_dim(terms, mine, 1, axis)
        send = lax.dynamic_slice_in_dim(terms, 1 - mine, 1, axis)
        total = keep.astype(jnp.float32) + swap(send, bit, count).astype(jnp.float32)
        terms = total if bit == order[-1] else total.astype(terms.dtype)
    return terms.reshape(terms.shape[-2:])


def by_core(left, count):
    parts = left.reshape(left.shape[0], count // 2, 2, left.shape[1] // count)
    core = own_bit(0)
    pick = lambda at: lax.dynamic_index_in_dim(parts, at, 2, keepdims=False).reshape(
        left.shape[0], left.shape[1] // 2
    )
    return (pick(core), pick(1 - core))


def pair_up(left, right, count):
    mine, other = by_core(left, count)
    return (
        jnp.concatenate([mine, swap(other, 0, count)], axis=0),
        jnp.concatenate([right, swap(right, 0, count)], axis=0),
    )


def summed_grad(left, right, pieces, count):
    levels = count.bit_length() - 1
    results = []
    offset = 0
    for extent, order in pieces:
        term = jnp.einsum(
            "tk,tw->kw",
            left,
            right[:, offset : offset + extent],
            preferred_element_type=jnp.float32,
        ).astype(jnp.bfloat16)
        term = term.reshape((2,) * (levels - 1) + (left.shape[1] * 2 // count, extent))
        results.append(halve(term, order, count, False))
        offset = offset + extent
    return results[0] if len(results) == 1 else jnp.concatenate(results, axis=1)


def body(
    inputs,
    live_keys,
    triple_weight,
    query_bias,
    value_bias,
    output_weight,
    output_bias,
    first_gain,
    first_shift,
    expand_weight,
    expand_bias,
    shrink_weight,
    shrink_bias,
    second_gain,
    second_shift,
    cotangent,
):
    count = lax.axis_size("fsdp")
    levels = count.bit_length() - 1
    width = inputs.shape[1]
    ways = orders(levels)
    vectors = (
        query_bias,
        value_bias,
        output_bias,
        first_gain,
        first_shift,
        expand_bias,
        shrink_bias,
        second_gain,
        second_shift,
    )
    packed = collect(jnp.concatenate(vectors)[None, :], ways[0], count)
    wide = []
    offset = 0
    for vector in vectors:
        wide.append(packed[:, offset : offset + vector.shape[0]].reshape(-1))
        offset = offset + vector.shape[0]
    gathered = (
        collect(triple_weight, ways[2], count),
        wide[0],
        wide[1],
        collect(output_weight, ways[0], count),
        wide[2],
        wide[3],
        wide[4],
        collect(expand_weight, ways[0], count),
        wide[5],
        collect(shrink_weight, ways[1], count),
        wide[6],
        wide[7],
        wide[8],
    )
    layer_out, saved = forward(gathered, inputs, live_keys)
    upper_small, upper_pairs, d_first = back_upper(gathered, saved, cotangent)
    lower_small, lower_pairs, input_grad = back_lower(gathered, saved, d_first)
    hidden = expand_weight.shape[1]
    shrink_grad = summed_grad(
        *pair_up(*upper_pairs[1], count),
        ((width * 3 // 4, ways[1]), (width // 4, ways[2])),
        count,
    )
    expand_grad = summed_grad(
        *pair_up(*upper_pairs[0], count),
        ((hidden * 3 // 4, ways[0]), (hidden // 4, ways[2])),
        count,
    )
    output_grad = summed_grad(*pair_up(*lower_pairs[1], count), ((width, ways[1]),), count)
    triple_grad = summed_grad(
        *pair_up(*lower_pairs[0], count),
        ((width, ways[0]), (width, ways[1]), (width, ways[2])),
        count,
    )
    sums = lower_small + upper_small
    terms = jnp.concatenate([item.reshape(count, -1) for item in sums], axis=1)
    terms = terms.reshape((2,) * levels + (1, terms.shape[1]))
    owned = halve(terms, list(range(levels)), count, True)[0]
    small = []
    offset = 0
    for item in sums:
        extent = item.shape[0] // count
        small.append(owned[offset : offset + extent])
        offset = offset + extent
    return (
        layer_out,
        input_grad,
        triple_grad,
        small[0],
        small[1],
        output_grad,
        small[2],
        small[3],
        small[4],
        expand_grad,
        small[5],
        shrink_grad,
        small[6],
        small[7],
        small[8],
    )


def solution(mesh):
    placed = (
        P("fsdp", None),
        P("fsdp"),
        P("fsdp", None),
        P("fsdp"),
        P("fsdp"),
        P("fsdp", None),
        P("fsdp"),
        P("fsdp"),
        P("fsdp"),
        P("fsdp", None),
        P("fsdp"),
        P("fsdp", None),
        P("fsdp"),
        P("fsdp"),
        P("fsdp"),
        P("fsdp", None),
    )
    return jax.shard_map(
        body,
        mesh=mesh,
        in_specs=placed,
        out_specs=(
            P("fsdp", None),
            P("fsdp", None),
            P("fsdp", None),
            P("fsdp"),
            P("fsdp"),
            P("fsdp", None),
            P("fsdp"),
            P("fsdp"),
            P("fsdp"),
            P("fsdp", None),
            P("fsdp"),
            P("fsdp", None),
            P("fsdp"),
            P("fsdp"),
            P("fsdp"),
        ),
        check_vma=False,
    )
```
